128 devices in a mesh: dp: 32 (over x, z, core), section: 4 (over y).
Axes of the slice: x: 4, y: 4, z: 4, core: 2. Of those that a mesh axis runs over, the one named last changes fastest.
Arguments:
- hidden: bfloat16 [12288, 4096], P('dp'), may hold values from -6 to 6
- encoded: bfloat16 [384, 128, 896], P('dp'), may hold values from -6 to 6
- owner: int32 [32, 12], P('dp'), may hold values from 0 to 5, never falling along the last dimension, each value on 1 to 4 neighbouring positions
- w_query: bfloat16 [4, 4096, 2048], P('section', 'dp'), may hold values from -0.09375 to 0.09375
- w_key: bfloat16 [4, 896, 2048], P('section'), may hold values from -0.1875 to 0.1875
- w_value: bfloat16 [4, 896, 2048], P('section'), may hold values from -0.1875 to 0.1875
- w_out: bfloat16 [4, 2048, 4096], P('section', None, 'dp'), may hold values from -0.75 to 0.75
Outputs:
- layer_outputs: bfloat16 [4, 12288, 4096], P('section', 'dp')
The draws below stay inside these ranges and needn't reach their ends.
Inputs may be any that keep to these rules, and one draw needn't show every extreme that they name: owner[g] lists for each of dp index g's 12 neighbours the span of g it was retrieved for; the list never falls, every span owns 1 to 4 neighbours and some span exactly 4.
All inputs are finite; a program needn't handle non-finite values.
Results may differ from the reference program's by a relative error of at most 0.028.
Values may be sent and summed in bfloat16 or wider, within the bound.
No kernel may reach another device: no remote copies, remote signals or barrier semaphores. Data moves between devices by JAX's collectives and lax.ppermute only.
A program may use at most 384 MiB of HBM per device.

```python
import math
import jax
import jax.numpy as jnp
import numpy as np
from jax import lax

D = 4096
HEADS = 16
HDIM = 128
ENC = 896
SPAN = 64
NBR_LEN = 128
MOST = 4
CH_DEV = 6
HD = 2048
SECTIONS = 4
GROUPS = 32
TOKENS = 12288
NBR_DEV = 12
NBRS = 384


def block_scale(own_key, extent, pieces, least, top_value):
    loudness, own = 1.0, jax.random.fold_in(own_key, 6)
    for axis_at, shards_of in pieces:
        heights = jnp.exp(jax.random.uniform(jax.random.fold_in(own, axis_at), (shards_of,), jnp.float32, least / len(pieces), top_value / len(pieces)))
        loudness = loudness * jnp.repeat(heights, extent[axis_at] // shards_of).reshape([-1 if axis == axis_at else 1 for axis in range(len(extent))])
    return loudness


def split_up(number_of, total, reach, skew):
    loads = [(1 << 20) // math.isqrt(rank ** skew) + 1 for rank in range(2, number_of + 1)]
    spare, holding = total - reach - (number_of - 1), [1] * (number_of - 1)
    while spare > 0:
        candidates = [i for i in range(number_of - 1) if holding[i] < reach]
        whole, left = sum([loads[i] for i in candidates]), spare
        for i in candidates:
            addition = min(reach - holding[i], max(1, left * loads[i] // whole), spare)
            holding[i] = holding[i] + addition
            spare = spare - addition
    return np.array([reach] + holding)


def uneven_parts(stream_key, count, total, limit, skew):
    if count == 2:
        one = jax.random.randint(stream_key, (), max(1, total - limit), min(limit, total - 1) + 1)
        return jnp.stack([one, total - one])
    tallies = jnp.asarray(split_up(count, total, limit, skew), jnp.int32)
    couples = (count - 1) // 2
    donor, taker = tallies[1:1 + 2 * couples:2], tallies[2:2 + 2 * couples:2]
    slack = jnp.minimum(donor - 1, limit - taker)
    shifted = jax.random.randint(jax.random.fold_in(stream_key, 1), (couples,), 0, 1 << 20) % (slack + 1)
    tallies = tallies.at[1:1 + 2 * couples:2].set(donor - shifted).at[2:2 + 2 * couples:2].set(taker + shifted)
    return tallies[jax.random.permutation(jax.random.fold_in(stream_key, 2), count)]


def noise(key, extent, spread, reach, split=(), kind=jnp.bfloat16):
    drawn = jax.random.normal(key, extent, jnp.float32) * spread
    if len(split) > 0:
        drawn = block_scale(key, extent, split, -0.22, 0.18) * drawn
    return jnp.clip(drawn, min=-reach, max=reach).astype(kind)


def setup_inputs(seed: int = 0) -> dict:
    arg_keys = jax.random.split(jax.random.key(seed), 8)
    hidden = noise(arg_keys[0], (TOKENS, D), 1.0, 6.0, ((0, 32),))
    encoded = noise(arg_keys[1], (NBRS, NBR_LEN, ENC), 1.0, 6.0, ((0, 32),))
    owner = jax.vmap(lambda own: jnp.searchsorted(jnp.cumsum(uneven_parts(own, CH_DEV, NBR_DEV, MOST, 2)), jnp.arange(NBR_DEV), side="right"))(jax.random.split(arg_keys[2], GROUPS)).reshape((GROUPS, NBR_DEV)).astype(jnp.int32)
    w_query = noise(arg_keys[3], (SECTIONS, D, HD), D ** -0.5, 0.09375, ((0, 4), (1, 32)))
    w_key = noise(arg_keys[4], (SECTIONS, ENC, HD), ENC ** -0.5, 0.1875, ((0, 4),))
    w_value = noise(arg_keys[5], (SECTIONS, ENC, HD), ENC ** -0.5, 0.1875, ((0, 4),))
    w_out = noise(arg_keys[6], (SECTIONS, HD, D), (HD // 32) ** -0.5, 0.75, ((0, 4), (2, 32)))
    return dict(hidden=hidden, encoded=encoded, owner=owner, w_query=w_query, w_key=w_key, w_value=w_value, w_out=w_out)


epsilon = 1e-05

def group_layer(stream, rows_enc, owners, query_mat, key_mat, value_mat, out_mat):
    widened = stream.astype(jnp.float32)
    normed = (widened * lax.rsqrt(lax.optimization_barrier(jnp.mean(widened * widened, axis=-1, keepdims=True)) + epsilon)).astype(jnp.bfloat16)
    queries = jnp.dot(normed, query_mat, preferred_element_type=jnp.float32).astype(jnp.bfloat16)
    key_rows = jnp.dot(rows_enc, key_mat, preferred_element_type=jnp.float32).astype(jnp.bfloat16)
    value_rows = jnp.dot(rows_enc, value_mat, preferred_element_type=jnp.float32).astype(jnp.bfloat16)
    span_count = stream.shape[0] // SPAN
    nbr_count = owners.shape[0]
    padding = jnp.zeros((MOST, NBR_LEN, HEADS, HDIM), jnp.bfloat16)
    key_blocks = jnp.concatenate([key_rows.reshape(nbr_count, NBR_LEN, HEADS, HDIM), padding], axis=0)
    value_blocks = jnp.concatenate([value_rows.reshape(nbr_count, NBR_LEN, HEADS, HDIM), padding], axis=0)
    span_ids = jnp.arange(span_count, dtype=jnp.int32)
    starts = lax.optimization_barrier(jnp.sum((owners[None, :] < span_ids[:, None]).astype(jnp.int32), axis=1)).astype(jnp.int32)
    counts = lax.optimization_barrier(jnp.sum((owners[None, :] == span_ids[:, None]).astype(jnp.int32), axis=1)).astype(jnp.int32)

    def window(blocks, offset):
        return lax.dynamic_slice_in_dim(blocks, offset.astype(jnp.int32), MOST, 0)
    near_keys = jax.vmap(window, (None, 0))(key_blocks, starts)
    near_values = jax.vmap(window, (None, 0))(value_blocks, starts)
    present = jnp.arange(MOST, dtype=jnp.int32)[None, :] < counts[:, None]
    query_heads = queries.reshape(span_count, SPAN, HEADS, HDIM).astype(jnp.float32)
    scores = jnp.einsum('cthd,cmlhd->chtml', query_heads, near_keys.astype(jnp.float32)) * (1.0 / HDIM ** 0.5)
    weights = jnp.where(present[:, None, None, :, None], jnp.exp(scores), 0.0)
    denominator = lax.optimization_barrier(jnp.sum(weights, axis=(3, 4), keepdims=True))
    weights_low = (weights / denominator).astype(jnp.bfloat16)
    attended = jnp.einsum('chtml,cmlhd->cthd', weights_low.astype(jnp.float32), near_values.astype(jnp.float32)).astype(jnp.bfloat16)
    branch = jnp.dot(attended.reshape(span_count * SPAN, HEADS * HDIM), out_mat, preferred_element_type=jnp.float32)
    return (widened + branch).astype(jnp.bfloat16)

def reference(hidden, encoded, owner, w_query, w_key, w_value, w_out):
    groups = owner.shape[0]
    streams = hidden.reshape(groups, -1, D)
    rows_enc = encoded.reshape(groups, -1, ENC)
    layers = []
    for section_at in range(SECTIONS):

        def apply_group(packed, section_at=section_at):
            return group_layer(packed[0], packed[1], packed[2], w_query[section_at], w_key[section_at], w_value[section_at], w_out[section_at])
        streams = lax.map(apply_group, (streams, rows_enc, owner))
        layers.append(streams.reshape(-1, D))
    return jnp.stack(layers)
```

```python
import functools

import jax
import jax.numpy as jnp
from jax import lax
from jax.experimental import pallas as pl
from jax.experimental.pallas import tpu as pltpu
from jax.sharding import PartitionSpec as P

HEADS = 16
HDIM = 128
SPAN = 64
NBR_LEN = 128
MOST = 4
SKEW = 2

epsilon = 1e-05


def step_kernel(
    step, tiles, plan, hidden_ref, moved_ref, weights_ref, keys_hbm, values_hbm, kept_in,
    sent_ref, kept_ref, stream, normed, queries, attended, keys, values, load_sems, store_sem,
):
    at = pl.program_id(0)
    half = tiles
    depth = weights_ref.shape[0] * weights_ref.shape[2]
    width = weights_ref.shape[3]
    span_at, active, first = plan[step, 0], plan[step, 1], plan[step, 2]
    window, low, high = plan[step, 3], plan[step, 4], plan[step, 5]
    window_rows = pl.ds(pl.multiple_of(window * NBR_LEN, NBR_LEN), MOST * NBR_LEN)
    key_copy = pltpu.make_async_copy(keys_hbm.at[window_rows, :], keys, load_sems.at[0])
    value_copy = pltpu.make_async_copy(values_hbm.at[window_rows, :], values, load_sems.at[1])

    @pl.when(at == 0)
    def _():
        key_copy.start()
        value_copy.start()
        total = jnp.zeros((SPAN, 1), jnp.float32)
        for tile in range(tiles):
            columns = slice(tile * depth, (tile + 1) * depth)
            piece = jnp.where(first == 1, hidden_ref[:, columns], moved_ref[:, columns])
            stream[tile] = piece
            wide = piece.astype(jnp.float32)
            total = total + jnp.sum(wide * wide, axis=1, keepdims=True)
        scale = lax.rsqrt(total / (tiles * depth) + epsilon)
        for tile in range(tiles):
            normed[tile] = (stream[tile].astype(jnp.float32) * scale).astype(jnp.bfloat16)

    @pl.when(at < half)
    def _():
        part = jnp.dot(
            normed[at], weights_ref[...].reshape(depth, width), preferred_element_type=jnp.float32
        )

        @pl.when(at == 0)
        def _():
            queries[...] = part

        @pl.when(at > 0)
        def _():
            queries[...] += part

    @pl.when(at == half - 1)
    def _():
        key_copy.wait()
        value_copy.wait()
        lane = lax.broadcasted_iota(jnp.int32, (SPAN, MOST * NBR_LEN), 1)
        belongs = (lane >= low * NBR_LEN) & (lane < high * NBR_LEN)
        for head in range(HEADS):
            columns = slice(head * HDIM, (head + 1) * HDIM)
            scores = lax.dot_general(
                queries[:, columns].astype(jnp.bfloat16),
                keys[:, columns],
                (((1,), (1,)), ((), ())),
                preferred_element_type=jnp.float32,
            ) * (1.0 / HDIM**0.5)
            weights = jnp.where(belongs, jnp.exp(scores), 0.0)
            weights = weights / jnp.sum(weights, axis=1, keepdims=True)
            attended[:, columns] = jnp.dot(
                weights.astype(jnp.bfloat16), values[:, columns], preferred_element_type=jnp.float32
            ).astype(jnp.bfloat16)

    @pl.when(at >= half)
    def _():
        tile = at - half
        branch = lax.dot_general(
            attended[...],
            weights_ref[...].reshape(depth, width),
            (((1,), (1,)), ((), ())),
            preferred_element_type=jnp.float32,
        )
        columns = pl.ds(pl.multiple_of(tile * depth, depth), depth)
        sent_ref[:, columns] = (stream[tile].astype(jnp.float32) + branch).astype(jnp.bfloat16)

    @pl.when((at == 2 * half - 1) & (active == 1))
    def _():
        rows = pl.ds(pl.multiple_of(span_at * SPAN, SPAN), SPAN)
        store = pltpu.make_async_copy(sent_ref, kept_ref.at[rows, :], store_sem)
        store.start()
        store.wait()


def layer_step(step, plan, hidden, moved, gathered, keys, values, kept, group=4):
    members, _, rows, width = gathered.shape
    tiles = members // group
    model_width = hidden.shape[1]
    depth = group * rows
    grid_spec = pltpu.PrefetchScalarGridSpec(
        num_scalar_prefetch=1,
        grid=(2 * tiles,),
        in_specs=[
            pl.BlockSpec((SPAN, model_width), lambda i, plan: (plan[step, 0], 0)),
            pl.BlockSpec((SPAN, model_width), lambda i, plan: (0, 0)),
            pl.BlockSpec((group, 1, rows, width), lambda i, plan: (i % tiles, i // tiles, 0, 0)),
            pl.BlockSpec(memory_space=pl.ANY),
            pl.BlockSpec(memory_space=pl.ANY),
            pl.BlockSpec(memory_space=pl.ANY),
        ],
        out_specs=[
            pl.BlockSpec((SPAN, model_width), lambda i, plan: (0, 0)),
            pl.BlockSpec(memory_space=pl.ANY),
        ],
        scratch_shapes=[
            pltpu.VMEM((tiles, SPAN, depth), jnp.bfloat16),
            pltpu.VMEM((tiles, SPAN, depth), jnp.bfloat16),
            pltpu.VMEM((SPAN, width), jnp.float32),
            pltpu.VMEM((SPAN, width), jnp.bfloat16),
            pltpu.VMEM((MOST * NBR_LEN, width), jnp.bfloat16),
            pltpu.VMEM((MOST * NBR_LEN, width), jnp.bfloat16),
            pltpu.SemaphoreType.DMA((2,)),
            pltpu.SemaphoreType.DMA,
        ],
    )
    work = 2 * SPAN * model_width * width * 2 + 2 * 2 * SPAN * MOST * NBR_LEN * width
    return pl.pallas_call(
        functools.partial(step_kernel, step, tiles),
        grid_spec=grid_spec,
        out_shape=[
            jax.ShapeDtypeStruct((SPAN, model_width), jnp.bfloat16),
            jax.ShapeDtypeStruct(kept.shape, kept.dtype),
        ],
        input_output_aliases={6: 1},
        compiler_params=pltpu.CompilerParams(
            dimension_semantics=("arbitrary",), vmem_limit_bytes=40 * 1024 * 1024
        ),
        cost_estimate=pl.CostEstimate(
            flops=work,
            bytes_accessed=gathered.size * 2 + 4 * MOST * NBR_LEN * width,
            transcendentals=SPAN * MOST * NBR_LEN * HEADS,
        ),
    )(plan, hidden, moved, gathered, keys, values, kept)


def make_plan(owners, section_id, steps, span_count):
    span = jnp.arange(steps, dtype=jnp.int32) - SKEW * section_id
    active = ((span >= 0) & (span < span_count)).astype(jnp.int32)
    span = jnp.clip(span, 0, span_count - 1)
    start = jnp.sum((owners[None, :] < span[:, None]).astype(jnp.int32), axis=1)
    count = jnp.sum((owners[None, :] == span[:, None]).astype(jnp.int32), axis=1)
    window = jnp.minimum(start, owners.shape[0] - MOST)
    low = start - window
    first = jnp.broadcast_to((section_id == 0).astype(jnp.int32), span.shape)
    return jnp.stack([span, active, first, window, low, low + count], axis=1).astype(jnp.int32)


def per_device(hidden, encoded, owner, w_query, w_key, w_value, w_out):
    section_id = lax.axis_index("section").astype(jnp.int32)
    sections = lax.axis_size("section")
    rows_enc = encoded.reshape(-1, encoded.shape[2])
    both = jnp.stack([w_query[0], w_out[0].T], axis=0)
    gathered = lax.all_gather(both, "dp", axis=0)
    keys = jnp.dot(rows_enc, w_key[0], preferred_element_type=jnp.float32).astype(jnp.bfloat16)
    values = jnp.dot(rows_enc, w_value[0], preferred_element_type=jnp.float32).astype(jnp.bfloat16)
    span_count = hidden.shape[0] // SPAN
    steps = span_count + SKEW * (sections - 1)
    plan = make_plan(owner[0], section_id, steps, span_count)
    route = [(s, s + 1) for s in range(sections - 1)]
    kept = jnp.zeros_like(hidden)
    arrived = [hidden[:SPAN]] * SKEW
    for step in range(steps):
        sent, kept = layer_step(
            step, plan, hidden, arrived[step], gathered, keys, values, kept
        )
        if step + SKEW < steps:
            arrived.append(lax.ppermute(sent, "section", route))
    return kept[None]


def solution(mesh):
    placed = (
        P("dp", None),
        P("dp", None, None),
        P("dp", None),
        P("section", "dp", None),
        P("section", None, None),
        P("section", None, None),
        P("section", None, "dp"),
    )
    return jax.shard_map(
        per_device, mesh=mesh, in_specs=placed, out_specs=P("section", "dp", None), check_vma=False
    )
```

```python
import functools

import jax
import jax.numpy as jnp
from jax import lax
from jax.experimental import pallas as pl
from jax.experimental.pallas import tpu as pltpu
from jax.sharding import PartitionSpec as P

HEADS = 16
HDIM = 128
SPAN = 64
NBR_LEN = 128
MOST = 4
VMEM_LIMIT = 14 * 1024 * 1024
PAIR = 2
SKEW = 2

epsilon = 1e-05


def pack_kernel(query_ref, out_ref, packed_ref):
    for head in range(HEADS):
        block = slice(head * HDIM, (head + 1) * HDIM)
        packed_ref[head] = query_ref[:, block]
        packed_ref[HEADS + head] = out_ref[block, :]


def pack(query_shard, out_shard):
    vmem = pl.BlockSpec(memory_space=pltpu.VMEM)
    return pl.pallas_call(
        pack_kernel,
        in_specs=[vmem, vmem],
        out_specs=vmem,
        out_shape=jax.ShapeDtypeStruct((2 * HEADS, HDIM, HDIM), query_shard.dtype),
    )(query_shard, out_shard)


def step_kernel(
    step, plan, hidden_hbm, moved_ref, mats, keys_hbm, values_hbm, kept_in,
    sent_ref, kept_ref, stream, normed, queries, attended, keys, values, load_sems, store_sem,
):
    members = mats.shape[0]
    depth, width = members * HDIM, HEADS * HDIM
    span_at, active, first = plan[step, 0], plan[step, 1], plan[step, 2]
    window, low, high = plan[step, 3], plan[step, 4], plan[step, 5]
    window_rows = pl.ds(pl.multiple_of(window * NBR_LEN, NBR_LEN), MOST * NBR_LEN)
    span_rows = pl.ds(pl.multiple_of(span_at * SPAN, SPAN), SPAN)
    key_copy = pltpu.make_async_copy(keys_hbm.at[window_rows, :], keys, load_sems.at[0])
    value_copy = pltpu.make_async_copy(values_hbm.at[window_rows, :], values, load_sems.at[1])
    hidden_copy = pltpu.make_async_copy(hidden_hbm.at[span_rows, :], stream, load_sems.at[2])
    hidden_copy.start()
    key_copy.start()
    value_copy.start()
    hidden_copy.wait()

    @pl.when(first == 0)
    def _():
        stream[...] = moved_ref[...]

    wide = stream[...].astype(jnp.float32)
    scale = lax.rsqrt(jnp.mean(wide * wide, axis=1, keepdims=True) + epsilon)
    normed[...] = (wide * scale).astype(jnp.bfloat16)
    lane = lax.broadcasted_iota(jnp.int32, (SPAN, MOST * NBR_LEN), 1)
    belongs = (lane >= low * NBR_LEN) & (lane < high * NBR_LEN)
    for head in range(0, HEADS, PAIR):
        matrix = jnp.concatenate(
            [mats[:, head + i].reshape(depth, HDIM) for i in range(PAIR)], axis=1
        )
        queries[:, head * HDIM : (head + PAIR) * HDIM] = jnp.dot(
            normed[...], matrix, preferred_element_type=jnp.float32
        ).astype(jnp.bfloat16)
    key_copy.wait()
    value_copy.wait()
    for head in range(HEADS):
        columns = slice(head * HDIM, (head + 1) * HDIM)
        scores = lax.dot_general(
            queries[:, columns],
            keys[:, columns],
            (((1,), (1,)), ((), ())),
            preferred_element_type=jnp.float32,
        ) * (1.0 / HDIM**0.5)
        weights = jnp.where(belongs, jnp.exp(scores), 0.0)
        weights = weights / jnp.sum(weights, axis=1, keepdims=True)
        attended[:, columns] = jnp.dot(
            weights.astype(jnp.bfloat16), values[:, columns], preferred_element_type=jnp.float32
        ).astype(jnp.bfloat16)
    for member in range(0, members, PAIR):
        matrix = jnp.concatenate(
            [mats[member + i, HEADS:].reshape(width, HDIM) for i in range(PAIR)], axis=1
        )
        branch = jnp.dot(attended[...], matrix, preferred_element_type=jnp.float32)
        columns = slice(member * HDIM, (member + PAIR) * HDIM)
        sent_ref[:, columns] = (stream[:, columns].astype(jnp.float32) + branch).astype(jnp.bfloat16)

    @pl.when(active == 1)
    def _():
        store = pltpu.make_async_copy(sent_ref, kept_ref.at[span_rows, :], store_sem)
        store.start()
        store.wait()


def layer_step(step, plan, hidden, moved, mats, keys, values, kept):
    model_width, width = hidden.shape[1], keys.shape[1]
    vmem = pl.BlockSpec(memory_space=pltpu.VMEM)
    smem = pl.BlockSpec(memory_space=pltpu.SMEM)
    anywhere = pl.BlockSpec(memory_space=pl.ANY)
    work = 2 * SPAN * model_width * width * 2 + 2 * 2 * SPAN * MOST * NBR_LEN * width
    return pl.pallas_call(
        functools.partial(step_kernel, step),
        in_specs=[smem, anywhere, vmem, vmem, anywhere, anywhere, anywhere],
        out_specs=[vmem, anywhere],
        scratch_shapes=[
            pltpu.VMEM((SPAN, model_width), jnp.bfloat16),
            pltpu.VMEM((SPAN, model_width), jnp.bfloat16),
            pltpu.VMEM((SPAN, width), jnp.bfloat16),
            pltpu.VMEM((SPAN, width), jnp.bfloat16),
            pltpu.VMEM((MOST * NBR_LEN, width), jnp.bfloat16),
            pltpu.VMEM((MOST * NBR_LEN, width), jnp.bfloat16),
            pltpu.SemaphoreType.DMA((3,)),
            pltpu.SemaphoreType.DMA,
        ],
        out_shape=[
            jax.ShapeDtypeStruct((SPAN, model_width), jnp.bfloat16),
            jax.ShapeDtypeStruct(kept.shape, kept.dtype),
        ],
        input_output_aliases={6: 1},
        compiler_params=pltpu.CompilerParams(vmem_limit_bytes=VMEM_LIMIT),
        cost_estimate=pl.CostEstimate(
            flops=work,
            bytes_accessed=20 * 1024 * 1024,
            transcendentals=SPAN * MOST * NBR_LEN * HEADS,
        ),
    )(plan, hidden, moved, pltpu.with_memory_space_constraint(mats, pltpu.VMEM), keys, values, kept)


def make_plan(owners, section_id, steps, span_count):
    span = jnp.arange(steps, dtype=jnp.int32) - SKEW * section_id
    active = ((span >= 0) & (span < span_count)).astype(jnp.int32)
    span = jnp.clip(span, 0, span_count - 1)
    start = jnp.sum((owners[None, :] < span[:, None]).astype(jnp.int32), axis=1)
    count = jnp.sum((owners[None, :] == span[:, None]).astype(jnp.int32), axis=1)
    window = jnp.minimum(start, owners.shape[0] - MOST)
    low = start - window
    first = jnp.broadcast_to((section_id == 0).astype(jnp.int32), span.shape)
    return jnp.stack([span, active, first, window, low, low + count], axis=1).astype(jnp.int32)


def per_device(hidden, encoded, owner, w_query, w_key, w_value, w_out):
    section_id = lax.axis_index("section").astype(jnp.int32)
    sections = lax.axis_size("section")
    rows_enc = encoded.reshape(-1, encoded.shape[2])
    mats = lax.all_gather(pack(w_query[0], w_out[0]), "dp", axis=0)
    keys = jnp.dot(rows_enc, w_key[0], preferred_element_type=jnp.float32).astype(jnp.bfloat16)
    values = jnp.dot(rows_enc, w_value[0], preferred_element_type=jnp.float32).astype(jnp.bfloat16)
    span_count = hidden.shape[0] // SPAN
    steps = span_count + SKEW * (sections - 1)
    plan = make_plan(owner[0], section_id, steps, span_count)
    route = [(s, s + 1) for s in range(sections - 1)]
    kept = jnp.zeros_like(hidden)
    arrived = [hidden[:SPAN]] * SKEW
    for step in range(steps):
        sent, kept = layer_step(
            step, plan, hidden, arrived[step], mats, keys, values, kept
        )
        if step + SKEW < steps:
            arrived.append(lax.ppermute(sent, "section", route))
    return kept[None]


def solution(mesh):
    placed = (
        P("dp", None),
        P("dp", None, None),
        P("dp", None),
        P("section", "dp", None),
        P("section", None, None),
        P("section", None, None),
        P("section", None, "dp"),
    )
    return jax.shard_map(
        per_device, mesh=mesh, in_specs=placed, out_specs=P("section", "dp", None), check_vma=False
    )
```

```python
import functools

import jax
import jax.numpy as jnp
from jax import lax
from jax.experimental import pallas as pl
from jax.experimental.pallas import tpu as pltpu
from jax.sharding import PartitionSpec as P

HEADS = 16
HDIM = 128
SPAN = 64
NBR_LEN = 128
MOST = 4
VMEM_LIMIT = 13 * 1024 * 1024
STORES = 4
PAIR = 2
SKEW = 2

epsilon = 1e-05


def pack_kernel(query_ref, out_ref, packed_ref):
    for head in range(HEADS):
        block = slice(head * HDIM, (head + 1) * HDIM)
        packed_ref[head] = query_ref[:, block]
        packed_ref[HEADS + head] = out_ref[block, :]


def pack(query_shard, out_shard):
    vmem = pl.BlockSpec(memory_space=pltpu.VMEM)
    return pl.pallas_call(
        pack_kernel,
        in_specs=[vmem, vmem],
        out_specs=vmem,
        out_shape=jax.ShapeDtypeStruct((2 * HEADS, HDIM, HDIM), query_shard.dtype),
    )(query_shard, out_shard)


def step_kernel(
    step, plan, hidden_ref, mats, keys_hbm, values_hbm, *rest,
):
    sent_ref, kept_ref, stream, queries, scores, attended, keys, values, load_sems, store_sems = rest[-10:]
    members = mats.shape[0]
    depth, width = members * HDIM, HEADS * HDIM
    span_at, active, first = plan[step, 0], plan[step, 1], plan[step, 2]
    window, low, high = plan[step, 3], plan[step, 4], plan[step, 5]
    window_at = pl.ds(pl.multiple_of(window * NBR_LEN, NBR_LEN), MOST * NBR_LEN)
    span_rows = pl.ds(pl.multiple_of(span_at * SPAN, SPAN), SPAN)
    key_copy = pltpu.make_async_copy(keys_hbm.at[:, window_at], keys, load_sems.at[0])
    value_copy = pltpu.make_async_copy(values_hbm.at[window_at, :], values, load_sems.at[1])
    key_copy.start()
    value_copy.start()

    if step < SKEW:
        stream[...] = hidden_ref[span_rows, :]
    else:
        moved_ref = rest[0]

        @pl.when(first == 1)
        def _():
            stream[...] = hidden_ref[span_rows, :]

        @pl.when(first == 0)
        def _():
            stream[...] = moved_ref[...]

    wide = stream[...].astype(jnp.float32)
    scale = lax.rsqrt(jnp.mean(wide * wide, axis=1, keepdims=True) + epsilon)
    for head in range(0, HEADS, PAIR):
        matrix = jnp.concatenate(
            [mats[:, head + i].reshape(depth, HDIM) for i in range(PAIR)], axis=1
        )
        part = jnp.dot(stream[...], matrix, preferred_element_type=jnp.float32)
        queries[:, head * HDIM : (head + PAIR) * HDIM] = (part * scale).astype(jnp.bfloat16)
    key_copy.wait()
    for head in range(HEADS):
        columns = slice(head * HDIM, (head + 1) * HDIM)
        scores[head] = jnp.dot(queries[:, columns], keys[columns, :], preferred_element_type=jnp.float32)
    value_copy.wait()
    lane = lax.broadcasted_iota(jnp.int32, (SPAN, MOST * NBR_LEN), 1)
    belongs = (lane >= low * NBR_LEN) & (lane < high * NBR_LEN)
    for head in range(HEADS):
        columns = slice(head * HDIM, (head + 1) * HDIM)
        weights = jnp.where(belongs, jnp.exp(scores[head] * (1.0 / HDIM**0.5)), 0.0)
        weights = weights / jnp.sum(weights, axis=1, keepdims=True)
        attended[:, columns] = jnp.dot(
            weights.astype(jnp.bfloat16), values[:, columns], preferred_element_type=jnp.float32
        ).astype(jnp.bfloat16)
    portion = depth // STORES
    stores = [
        pltpu.make_async_copy(
            sent_ref.at[:, i * portion : (i + 1) * portion],
            kept_ref.at[span_rows, i * portion : (i + 1) * portion],
            store_sems.at[i],
        )
        for i in range(STORES)
    ]
    for member in range(0, members, PAIR):
        matrix = jnp.concatenate(
            [mats[member + i, HEADS:].reshape(width, HDIM) for i in range(PAIR)], axis=1
        )
        branch = jnp.dot(attended[...], matrix, preferred_element_type=jnp.float32)
        columns = slice(member * HDIM, (member + PAIR) * HDIM)
        sent_ref[:, columns] = (stream[:, columns].astype(jnp.float32) + branch).astype(jnp.bfloat16)
        if columns.stop % portion == 0:
            pl.when(active == 1)(stores[columns.stop // portion - 1].start)

    @pl.when(active == 1)
    def _():
        for store in stores:
            store.wait()


def layer_step(step, plan, hidden, moved, mats, keys, values, kept):
    model_width, width = hidden.shape[1], values.shape[1]
    vmem = pl.BlockSpec(memory_space=pltpu.VMEM)
    smem = pl.BlockSpec(memory_space=pltpu.SMEM)
    anywhere = pl.BlockSpec(memory_space=pl.ANY)
    work = 2 * SPAN * model_width * width * 2 + 2 * 2 * SPAN * MOST * NBR_LEN * width
    arrived = [] if moved is None else [moved]
    before = [] if kept is None else [kept]
    return pl.pallas_call(
        functools.partial(step_kernel, step),
        in_specs=[smem, vmem, vmem, anywhere, anywhere] + [vmem] * len(arrived) + [anywhere] * len(before),
        out_specs=[vmem, anywhere],
        scratch_shapes=[
            pltpu.VMEM((SPAN, model_width), jnp.bfloat16),
            pltpu.VMEM((SPAN, width), jnp.bfloat16),
            pltpu.VMEM((HEADS, SPAN, MOST * NBR_LEN), jnp.float32),
            pltpu.VMEM((SPAN, width), jnp.bfloat16),
            pltpu.VMEM((width, MOST * NBR_LEN), jnp.bfloat16),
            pltpu.VMEM((MOST * NBR_LEN, width), jnp.bfloat16),
            pltpu.SemaphoreType.DMA((2,)),
            pltpu.SemaphoreType.DMA((STORES,)),
        ],
        out_shape=[
            jax.ShapeDtypeStruct((SPAN, model_width), jnp.bfloat16),
            jax.ShapeDtypeStruct(hidden.shape, hidden.dtype),
        ],
        input_output_aliases={5 + len(arrived): 1} if before else {},
        compiler_params=pltpu.CompilerParams(vmem_limit_bytes=VMEM_LIMIT),
        cost_estimate=pl.CostEstimate(
            flops=work,
            bytes_accessed=20 * 1024 * 1024,
            transcendentals=SPAN * MOST * NBR_LEN * HEADS,
        ),
    )(
        plan,
        pltpu.with_memory_space_constraint(hidden, pltpu.VMEM),
        pltpu.with_memory_space_constraint(mats, pltpu.VMEM),
        pltpu.with_memory_space_constraint(keys, pltpu.HBM),
        pltpu.with_memory_space_constraint(values, pltpu.HBM),
        *arrived,
        *before,
    )


def make_plan(owners, section_id, steps, span_count):
    span = jnp.arange(steps, dtype=jnp.int32) - SKEW * section_id
    active = ((span >= 0) & (span < span_count)).astype(jnp.int32)
    span = jnp.clip(span, 0, span_count - 1)
    start = jnp.sum((owners[None, :] < span[:, None]).astype(jnp.int32), axis=1)
    count = jnp.sum((owners[None, :] == span[:, None]).astype(jnp.int32), axis=1)
    window = jnp.minimum(start, owners.shape[0] - MOST)
    low = start - window
    first = jnp.broadcast_to((section_id == 0).astype(jnp.int32), span.shape)
    return jnp.stack([span, active, first, window, low, low + count], axis=1).astype(jnp.int32)


def per_device(hidden, encoded, owner, w_query, w_key, w_value, w_out):
    section_id = lax.axis_index("section").astype(jnp.int32)
    sections = lax.axis_size("section")
    rows_enc = encoded.reshape(-1, encoded.shape[2])
    mats = lax.all_gather(pack(w_query[0], w_out[0]), "dp", axis=0)
    keys = lax.dot_general(
        w_key[0], rows_enc, (((0,), (1,)), ((), ())), preferred_element_type=jnp.float32
    ).astype(jnp.bfloat16)
    values = jnp.dot(rows_enc, w_value[0], preferred_element_type=jnp.float32).astype(jnp.bfloat16)
    span_count = hidden.shape[0] // SPAN
    steps = span_count + SKEW * (sections - 1)
    plan = make_plan(owner[0], section_id, steps, span_count)
    route = [(s, s + 1) for s in range(sections - 1)]
    kept = None
    arrived = [None] * SKEW
    for step in range(steps):
        sent, kept = layer_step(
            step, plan, hidden, arrived[step], mats, keys, values, kept
        )
        if step + SKEW < steps:
            arrived.append(lax.ppermute(sent, "section", route))
    return kept[None]


def solution(mesh):
    placed = (
        P("dp", None),
        P("dp", None, None),
        P("dp", None),
        P("section", "dp", None),
        P("section", None, None),
        P("section", None, None),
        P("section", None, "dp"),
    )
    return jax.shard_map(
        per_device, mesh=mesh, in_specs=placed, out_specs=P("section", "dp", None), check_vma=False
    )
```

```python
import functools

import jax
import jax.numpy as jnp
from jax import lax
from jax.experimental import pallas as pl
from jax.experimental.pallas import tpu as pltpu
from jax.sharding import PartitionSpec as P

HEADS = 16
HDIM = 128
SPAN = 64
NBR_LEN = 128
MOST = 4
VMEM_LIMIT = 13 * 1024 * 1024
LOT = 6
KEPT = HEADS - 2 * LOT
RING = 4
CORES = 2
NEAR = [0, -1, 1, 2]
STORES = 4
PAIR = 2
SKEW = 2

epsilon = 1e-05


def pack_kernel(query_ref, out_ref, packed_ref, first_ref, second_ref):
    for head in range(HEADS):
        block = slice(head * HDIM, (head + 1) * HDIM)
        if head < KEPT:
            packed_ref[head] = query_ref[:, block]
        elif head < KEPT + LOT:
            first_ref[head - KEPT] = query_ref[:, block]
        else:
            second_ref[head - KEPT - LOT] = query_ref[:, block]
        packed_ref[KEPT + head] = out_ref[block, :]


def pack(query_shard, out_shard):
    vmem = pl.BlockSpec(memory_space=pltpu.VMEM)
    shapes = [(KEPT + HEADS, HDIM, HDIM), (LOT, HDIM, HDIM), (LOT, HDIM, HDIM)]
    return pl.pallas_call(
        pack_kernel,
        in_specs=[vmem, vmem],
        out_specs=[vmem] * 3,
        out_shape=[jax.ShapeDtypeStruct(shape, query_shard.dtype) for shape in shapes],
    )(query_shard, out_shard)


def shifted(block, x_by, z_by, core_by=0):
    route = []
    for x in range(RING):
        for z in range(RING):
            for core in range(CORES):
                there = ((x + x_by) % RING * RING + (z + z_by) % RING) * CORES + (core ^ core_by)
                route.append(((x * RING + z) * CORES + core, there))
    return lax.ppermute(block, "dp", route)


def around(block, x_by, z_by):
    half = block.shape[0] // 2
    behind = shifted(block, x_by, z_by)
    ahead = shifted(block, -x_by, -z_by)
    far_first = shifted(behind[:half], x_by, z_by)
    far_second = shifted(ahead[half:], -x_by, -z_by)
    return jnp.concatenate([block, behind, ahead, far_first, far_second], axis=0)


def gather_lots(first, second):
    first_row, second_row = around(first, 1, 0), around(second, 0, 1)
    lots = [around(first_row, 0, 1), around(second_row, 1, 0)]
    lots = [lot.reshape(RING * RING, LOT, HDIM, HDIM) for lot in lots]
    return lots + [shifted(lot, 0, 0, 1) for lot in lots]


def place_kernel(table, *refs):
    lots, placed, sems = refs[:4], refs[4], refs[5]
    copies = []
    for which, lot in enumerate(lots):
        for member in range(RING * RING):
            heads = pl.ds(which % 2 * LOT, LOT)
            copies.append(
                pltpu.make_async_copy(
                    lot.at[member], placed.at[table[which, member], heads], sems.at[which, member]
                )
            )
            copies[-1].start()
    for copy in copies:
        copy.wait()


def place(lots):
    me = lax.axis_index("dp").astype(jnp.int32)
    x, z, core = me // (RING * CORES), me // CORES % RING, me % CORES
    near = jnp.array(NEAR, jnp.int32)
    x_at, z_at = (x + near + RING) % RING, (z + near + RING) % RING
    rows = []
    for core_by in range(CORES):
        core_at = (core + core_by) % CORES
        first = (x_at[None, :] * RING + z_at[:, None]) * CORES + core_at
        second = (x_at[:, None] * RING + z_at[None, :]) * CORES + core_at
        rows += [first.reshape(-1), second.reshape(-1)]
    anywhere = pl.BlockSpec(memory_space=pl.ANY)
    return pl.pallas_call(
        place_kernel,
        in_specs=[pl.BlockSpec(memory_space=pltpu.SMEM)] + [anywhere] * 4,
        out_specs=anywhere,
        out_shape=jax.ShapeDtypeStruct((RING * RING * CORES, 2 * LOT, HDIM, HDIM), jnp.bfloat16),
        scratch_shapes=[pltpu.SemaphoreType.DMA((4, RING * RING))],
        cost_estimate=pl.CostEstimate(flops=0, bytes_accessed=24 * 1024 * 1024, transcendentals=0),
    )(jnp.stack(rows).astype(jnp.int32), *lots)


def step_kernel(
    step, plan, hidden_ref, mats, more, keys_hbm, values_hbm, *rest,
):
    sent_ref, kept_ref, stream, queries, scores, attended, keys, values, load_sems, store_sems = rest[-10:]
    members = mats.shape[0]
    depth, width = members * HDIM, HEADS * HDIM
    span_at, active, first = plan[step, 0], plan[step, 1], plan[step, 2]
    window, low, high = plan[step, 3], plan[step, 4], plan[step, 5]
    window_at = pl.ds(pl.multiple_of(window * NBR_LEN, NBR_LEN), MOST * NBR_LEN)
    span_rows = pl.ds(pl.multiple_of(span_at * SPAN, SPAN), SPAN)
    key_copy = pltpu.make_async_copy(keys_hbm.at[:, window_at], keys, load_sems.at[0])
    value_copy = pltpu.make_async_copy(values_hbm.at[window_at, :], values, load_sems.at[1])
    key_copy.start()
    value_copy.start()

    if step < SKEW:
        stream[...] = hidden_ref[span_rows, :]
    else:
        moved_ref = rest[0]

        @pl.when(first == 1)
        def _():
            stream[...] = hidden_ref[span_rows, :]

        @pl.when(first == 0)
        def _():
            stream[...] = moved_ref[...]

    wide = stream[...].astype(jnp.float32)
    scale = lax.rsqrt(jnp.mean(wide * wide, axis=1, keepdims=True) + epsilon)
    for head in range(0, HEADS, PAIR):
        source, at = (mats, head) if head < KEPT else (more, head - KEPT)
        matrix = jnp.concatenate(
            [source[:, at + i].reshape(depth, HDIM) for i in range(PAIR)], axis=1
        )
        part = jnp.dot(stream[...], matrix, preferred_element_type=jnp.float32)
        queries[:, head * HDIM : (head + PAIR) * HDIM] = (part * scale).astype(jnp.bfloat16)
    key_copy.wait()
    for head in range(HEADS):
        columns = slice(head * HDIM, (head + 1) * HDIM)
        scores[head] = jnp.dot(queries[:, columns], keys[columns, :], preferred_element_type=jnp.float32)
    value_copy.wait()
    lane = lax.broadcasted_iota(jnp.int32, (SPAN, MOST * NBR_LEN), 1)
    belongs = (lane >= low * NBR_LEN) & (lane < high * NBR_LEN)
    for head in range(HEADS):
        columns = slice(head * HDIM, (head + 1) * HDIM)
        weights = jnp.where(belongs, jnp.exp(scores[head] * (1.0 / HDIM**0.5)), 0.0)
        weights = weights / jnp.sum(weights, axis=1, keepdims=True)
        attended[:, columns] = jnp.dot(
            weights.astype(jnp.bfloat16), values[:, columns], preferred_element_type=jnp.float32
        ).astype(jnp.bfloat16)
    portion = depth // STORES
    stores = [
        pltpu.make_async_copy(
            sent_ref.at[:, i * portion : (i + 1) * portion],
            kept_ref.at[span_rows, i * portion : (i + 1) * portion],
            store_sems.at[i],
        )
        for i in range(STORES)
    ]
    for member in range(0, members, PAIR):
        matrix = jnp.concatenate(
            [mats[member + i, KEPT:].reshape(width, HDIM) for i in range(PAIR)], axis=1
        )
        branch = jnp.dot(attended[...], matrix, preferred_element_type=jnp.float32)
        columns = slice(member * HDIM, (member + PAIR) * HDIM)
        sent_ref[:, columns] = (stream[:, columns].astype(jnp.float32) + branch).astype(jnp.bfloat16)
        if columns.stop % portion == 0:
            pl.when(active == 1)(stores[columns.stop // portion - 1].start)

    @pl.when(active == 1)
    def _():
        for store in stores:
            store.wait()


def layer_step(step, plan, hidden, moved, mats, more, keys, values, kept):
    model_width, width = hidden.shape[1], values.shape[1]
    vmem = pl.BlockSpec(memory_space=pltpu.VMEM)
    smem = pl.BlockSpec(memory_space=pltpu.SMEM)
    anywhere = pl.BlockSpec(memory_space=pl.ANY)
    work = 2 * SPAN * model_width * width * 2 + 2 * 2 * SPAN * MOST * NBR_LEN * width
    arrived = [] if moved is None else [moved]
    before = [] if kept is None else [kept]
    return pl.pallas_call(
        functools.partial(step_kernel, step),
        in_specs=[smem, vmem, vmem, vmem, anywhere, anywhere] + [vmem] * len(arrived) + [anywhere] * len(before),
        out_specs=[vmem, anywhere],
        scratch_shapes=[
            pltpu.VMEM((SPAN, model_width), jnp.bfloat16),
            pltpu.VMEM((SPAN, width), jnp.bfloat16),
            pltpu.VMEM((HEADS, SPAN, MOST * NBR_LEN), jnp.float32),
            pltpu.VMEM((SPAN, width), jnp.bfloat16),
            pltpu.VMEM((width, MOST * NBR_LEN), jnp.bfloat16),
            pltpu.VMEM((MOST * NBR_LEN, width), jnp.bfloat16),
            pltpu.SemaphoreType.DMA((2,)),
            pltpu.SemaphoreType.DMA((STORES,)),
        ],
        out_shape=[
            jax.ShapeDtypeStruct((SPAN, model_width), jnp.bfloat16),
            jax.ShapeDtypeStruct(hidden.shape, hidden.dtype),
        ],
        input_output_aliases={6 + len(arrived): 1} if before else {},
        compiler_params=pltpu.CompilerParams(vmem_limit_bytes=VMEM_LIMIT),
        cost_estimate=pl.CostEstimate(
            flops=work,
            bytes_accessed=20 * 1024 * 1024,
            transcendentals=SPAN * MOST * NBR_LEN * HEADS,
        ),
    )(
        plan,
        pltpu.with_memory_space_constraint(hidden, pltpu.VMEM),
        pltpu.with_memory_space_constraint(mats, pltpu.VMEM),
        pltpu.with_memory_space_constraint(more, pltpu.VMEM),
        pltpu.with_memory_space_constraint(keys, pltpu.HBM),
        pltpu.with_memory_space_constraint(values, pltpu.HBM),
        *arrived,
        *before,
    )


def make_plan(owners, section_id, steps, span_count):
    span = jnp.arange(steps, dtype=jnp.int32) - SKEW * section_id
    active = ((span >= 0) & (span < span_count)).astype(jnp.int32)
    span = jnp.clip(span, 0, span_count - 1)
    start = jnp.sum((owners[None, :] < span[:, None]).astype(jnp.int32), axis=1)
    count = jnp.sum((owners[None, :] == span[:, None]).astype(jnp.int32), axis=1)
    window = jnp.minimum(start, owners.shape[0] - MOST)
    low = start - window
    first = jnp.broadcast_to((section_id == 0).astype(jnp.int32), span.shape)
    return jnp.stack([span, active, first, window, low, low + count], axis=1).astype(jnp.int32)


def per_device(hidden, encoded, owner, w_query, w_key, w_value, w_out):
    section_id = lax.axis_index("section").astype(jnp.int32)
    sections = lax.axis_size("section")
    rows_enc = encoded.reshape(-1, encoded.shape[2])
    packed, first, second = pack(w_query[0], w_out[0])
    mats = lax.all_gather(packed, "dp", axis=0)
    more = place(gather_lots(first, second))
    keys = lax.dot_general(
        w_key[0], rows_enc, (((0,), (1,)), ((), ())), preferred_element_type=jnp.float32
    ).astype(jnp.bfloat16)
    values = jnp.dot(rows_enc, w_value[0], preferred_element_type=jnp.float32).astype(jnp.bfloat16)
    span_count = hidden.shape[0] // SPAN
    steps = span_count + SKEW * (sections - 1)
    plan = make_plan(owner[0], section_id, steps, span_count)
    route = [(s, s + 1) for s in range(sections - 1)]
    kept = None
    arrived = [None] * SKEW
    for step in range(steps):
        sent, kept = layer_step(
            step, plan, hidden, arrived[step], mats, more, keys, values, kept
        )
        if step + SKEW < steps:
            arrived.append(lax.ppermute(sent, "section", route))
    return kept[None]


def solution(mesh):
    placed = (
        P("dp", None),
        P("dp", None, None),
        P("dp", None),
        P("section", "dp", None),
        P("section", None, None),
        P("section", None, None),
        P("section", None, "dp"),
    )
    return jax.shard_map(
        per_device, mesh=mesh, in_specs=placed, out_specs=P("section", "dp", None), check_vma=False
    )
```

```python
import functools

import jax
import jax.numpy as jnp
from jax import lax
from jax.experimental import pallas as pl
from jax.experimental.pallas import tpu as pltpu
from jax.sharding import PartitionSpec as P

HEADS = 16
HDIM = 128
SPAN = 64
NBR_LEN = 128
MOST = 4
VMEM_LIMIT = 13 * 1024 * 1024
LOT = 6
KEPT = HEADS - 2 * LOT
RING = 4
CORES = 2
NEAR = [0, -1, 1, 2]
STORES = 4
PAIR = 2
SKEW = 2

epsilon = 1e-05


def pack_kernel(query_ref, out_ref, packed_ref, first_ref, second_ref):
    for head in range(HEADS):
        block = slice(head * HDIM, (head + 1) * HDIM)
        if head < KEPT:
            packed_ref[head] = query_ref[:, block]
        elif head < KEPT + LOT:
            first_ref[head - KEPT] = query_ref[:, block]
        else:
            second_ref[head - KEPT - LOT] = query_ref[:, block]
        packed_ref[KEPT + head] = out_ref[block, :]


def pack(query_shard, out_shard):
    vmem = pl.BlockSpec(memory_space=pltpu.VMEM)
    shapes = [(KEPT + HEADS, HDIM, HDIM), (LOT, HDIM, HDIM), (LOT, HDIM, HDIM)]
    return pl.pallas_call(
        pack_kernel,
        in_specs=[vmem, vmem],
        out_specs=[vmem] * 3,
        out_shape=[jax.ShapeDtypeStruct(shape, query_shard.dtype) for shape in shapes],
    )(query_shard, out_shard)


def shifted(block, x_by, z_by, core_by=0):
    route = []
    for x in range(RING):
        for z in range(RING):
            for core in range(CORES):
                there = ((x + x_by) % RING * RING + (z + z_by) % RING) * CORES + (core ^ core_by)
                route.append(((x * RING + z) * CORES + core, there))
    return lax.ppermute(block, "dp", route)


def around(block, x_by, z_by, meanwhile=None):
    half = block.shape[0] // 2
    behind = shifted(block, x_by, z_by)
    ahead = shifted(block, -x_by, -z_by)
    if meanwhile is not None:
        behind, ahead, meanwhile = lax.optimization_barrier((behind, ahead, meanwhile))
    far_first = shifted(behind[:half], x_by, z_by)
    far_second = shifted(ahead[half:], -x_by, -z_by)
    joined = jnp.concatenate([block, behind, ahead, far_first, far_second], axis=0)
    return joined if meanwhile is None else (joined, meanwhile)


def gather_lots(first, second, meanwhile):
    first_row, second_row = around(first, 1, 0), around(second, 0, 1)
    first_lot, meanwhile = around(first_row, 0, 1, meanwhile)
    lots = [first_lot, around(second_row, 1, 0)]
    lots = [lot.reshape(RING * RING, LOT, HDIM, HDIM) for lot in lots]
    return lots + [shifted(lot, 0, 0, 1) for lot in lots], meanwhile


def place_kernel(table, *refs):
    lots, placed, held, load_sems, sems = refs[:4], refs[4], refs[5], refs[6], refs[7]
    loads = [pltpu.make_async_copy(lot, held.at[i], load_sems.at[i]) for i, lot in enumerate(lots)]
    for load in loads:
        load.start()
    copies = []
    for which, load in enumerate(loads):
        load.wait()
        for member in range(RING * RING):
            heads = pl.ds(which % 2 * LOT, LOT)
            copies.append(
                pltpu.make_async_copy(
                    held.at[which, member],
                    placed.at[table[which, member], heads],
                    sems.at[which, member],
                )
            )
            copies[-1].start()
    for copy in copies:
        copy.wait()


def place(lots):
    me = lax.axis_index("dp").astype(jnp.int32)
    x, z, core = me // (RING * CORES), me // CORES % RING, me % CORES
    near = jnp.array(NEAR, jnp.int32)
    x_at, z_at = (x + near + RING) % RING, (z + near + RING) % RING
    rows = []
    for core_by in range(CORES):
        core_at = (core + core_by) % CORES
        first = (x_at[None, :] * RING + z_at[:, None]) * CORES + core_at
        second = (x_at[:, None] * RING + z_at[None, :]) * CORES + core_at
        rows += [first.reshape(-1), second.reshape(-1)]
    anywhere = pl.BlockSpec(memory_space=pl.ANY)
    return pl.pallas_call(
        place_kernel,
        in_specs=[pl.BlockSpec(memory_space=pltpu.SMEM)] + [anywhere] * 4,
        out_specs=anywhere,
        out_shape=jax.ShapeDtypeStruct((RING * RING * CORES, 2 * LOT, HDIM, HDIM), jnp.bfloat16),
        scratch_shapes=[
            pltpu.VMEM((4, *lots[0].shape), lots[0].dtype),
            pltpu.SemaphoreType.DMA((4,)),
            pltpu.SemaphoreType.DMA((4, RING * RING)),
        ],
        compiler_params=pltpu.CompilerParams(vmem_limit_bytes=16 * 1024 * 1024),
        cost_estimate=pl.CostEstimate(flops=0, bytes_accessed=24 * 1024 * 1024, transcendentals=0),
    )(jnp.stack(rows).astype(jnp.int32), *lots)


def step_kernel(
    step, plan, hidden_ref, mats, more, keys_hbm, values_hbm, *rest,
):
    sent_ref, kept_ref, stream, queries, scores, attended, keys, values, load_sems, store_sems = rest[-10:]
    members = mats.shape[0]
    depth, width = members * HDIM, HEADS * HDIM
    span_at, active, first = plan[step, 0], plan[step, 1], plan[step, 2]
    window, low, high = plan[step, 3], plan[step, 4], plan[step, 5]
    window_at = pl.ds(pl.multiple_of(window * NBR_LEN, NBR_LEN), MOST * NBR_LEN)
    span_rows = pl.ds(pl.multiple_of(span_at * SPAN, SPAN), SPAN)
    key_copy = pltpu.make_async_copy(keys_hbm.at[:, window_at], keys, load_sems.at[0])
    value_copy = pltpu.make_async_copy(values_hbm.at[window_at, :], values, load_sems.at[1])
    key_copy.start()
    value_copy.start()

    if step < SKEW:
        stream[...] = hidden_ref[span_rows, :]
    else:
        moved_ref = rest[0]

        @pl.when(first == 1)
        def _():
            stream[...] = hidden_ref[span_rows, :]

        @pl.when(first == 0)
        def _():
            stream[...] = moved_ref[...]

    wide = stream[...].astype(jnp.float32)
    scale = lax.rsqrt(jnp.mean(wide * wide, axis=1, keepdims=True) + epsilon)
    for head in range(0, HEADS, PAIR):
        source, at = (mats, head) if head < KEPT else (more, head - KEPT)
        matrix = jnp.concatenate(
            [source[:, at + i].reshape(depth, HDIM) for i in range(PAIR)], axis=1
        )
        part = jnp.dot(stream[...], matrix, preferred_element_type=jnp.float32)
        queries[:, head * HDIM : (head + PAIR) * HDIM] = (part * scale).astype(jnp.bfloat16)
    key_copy.wait()
    for head in range(HEADS):
        columns = slice(head * HDIM, (head + 1) * HDIM)
        scores[head] = jnp.dot(queries[:, columns], keys[columns, :], preferred_element_type=jnp.float32)
    value_copy.wait()
    lane = lax.broadcasted_iota(jnp.int32, (SPAN, MOST * NBR_LEN), 1)
    belongs = (lane >= low * NBR_LEN) & (lane < high * NBR_LEN)
    for head in range(HEADS):
        columns = slice(head * HDIM, (head + 1) * HDIM)
        weights = jnp.where(belongs, jnp.exp(scores[head] * (1.0 / HDIM**0.5)), 0.0)
        weights = weights / jnp.sum(weights, axis=1, keepdims=True)
        attended[:, columns] = jnp.dot(
            weights.astype(jnp.bfloat16), values[:, columns], preferred_element_type=jnp.float32
        ).astype(jnp.bfloat16)
    portion = depth // STORES
    stores = [
        pltpu.make_async_copy(
            sent_ref.at[:, i * portion : (i + 1) * portion],
            kept_ref.at[span_rows, i * portion : (i + 1) * portion],
            store_sems.at[i],
        )
        for i in range(STORES)
    ]
    for member in range(0, members, PAIR):
        matrix = jnp.concatenate(
            [mats[member + i, KEPT:].reshape(width, HDIM) for i in range(PAIR)], axis=1
        )
        branch = jnp.dot(attended[...], matrix, preferred_element_type=jnp.float32)
        columns = slice(member * HDIM, (member + PAIR) * HDIM)
        sent_ref[:, columns] = (stream[:, columns].astype(jnp.float32) + branch).astype(jnp.bfloat16)
        if columns.stop % portion == 0:
            pl.when(active == 1)(stores[columns.stop // portion - 1].start)

    @pl.when(active == 1)
    def _():
        for store in stores:
            store.wait()


def layer_step(step, plan, hidden, moved, mats, more, keys, values, kept):
    model_width, width = hidden.shape[1], values.shape[1]
    vmem = pl.BlockSpec(memory_space=pltpu.VMEM)
    smem = pl.BlockSpec(memory_space=pltpu.SMEM)
    anywhere = pl.BlockSpec(memory_space=pl.ANY)
    work = 2 * SPAN * model_width * width * 2 + 2 * 2 * SPAN * MOST * NBR_LEN * width
    arrived = [] if moved is None else [moved]
    before = [] if kept is None else [kept]
    return pl.pallas_call(
        functools.partial(step_kernel, step),
        in_specs=[smem, vmem, vmem, vmem, anywhere, anywhere] + [vmem] * len(arrived) + [anywhere] * len(before),
        out_specs=[vmem, anywhere],
        scratch_shapes=[
            pltpu.VMEM((SPAN, model_width), jnp.bfloat16),
            pltpu.VMEM((SPAN, width), jnp.bfloat16),
            pltpu.VMEM((HEADS, SPAN, MOST * NBR_LEN), jnp.float32),
            pltpu.VMEM((SPAN, width), jnp.bfloat16),
            pltpu.VMEM((width, MOST * NBR_LEN), jnp.bfloat16),
            pltpu.VMEM((MOST * NBR_LEN, width), jnp.bfloat16),
            pltpu.SemaphoreType.DMA((2,)),
            pltpu.SemaphoreType.DMA((STORES,)),
        ],
        out_shape=[
            jax.ShapeDtypeStruct((SPAN, model_width), jnp.bfloat16),
            jax.ShapeDtypeStruct(hidden.shape, hidden.dtype),
        ],
        input_output_aliases={6 + len(arrived): 1} if before else {},
        compiler_params=pltpu.CompilerParams(vmem_limit_bytes=VMEM_LIMIT),
        cost_estimate=pl.CostEstimate(
            flops=work,
            bytes_accessed=20 * 1024 * 1024,
            transcendentals=SPAN * MOST * NBR_LEN * HEADS,
        ),
    )(
        plan,
        pltpu.with_memory_space_constraint(hidden, pltpu.VMEM),
        pltpu.with_memory_space_constraint(mats, pltpu.VMEM),
        pltpu.with_memory_space_constraint(more, pltpu.VMEM),
        pltpu.with_memory_space_constraint(keys, pltpu.HBM),
        pltpu.with_memory_space_constraint(values, pltpu.HBM),
        *arrived,
        *before,
    )


def make_plan(owners, section_id, steps, span_count):
    span = jnp.arange(steps, dtype=jnp.int32) - SKEW * section_id
    active = ((span >= 0) & (span < span_count)).astype(jnp.int32)
    span = jnp.clip(span, 0, span_count - 1)
    start = jnp.sum((owners[None, :] < span[:, None]).astype(jnp.int32), axis=1)
    count = jnp.sum((owners[None, :] == span[:, None]).astype(jnp.int32), axis=1)
    window = jnp.minimum(start, owners.shape[0] - MOST)
    low = start - window
    first = jnp.broadcast_to((section_id == 0).astype(jnp.int32), span.shape)
    return jnp.stack([span, active, first, window, low, low + count], axis=1).astype(jnp.int32)


def per_device(hidden, encoded, owner, w_query, w_key, w_value, w_out):
    section_id = lax.axis_index("section").astype(jnp.int32)
    sections = lax.axis_size("section")
    rows_enc = encoded.reshape(-1, encoded.shape[2])
    packed, first, second = pack(w_query[0], w_out[0])
    mats = lax.all_gather(packed, "dp", axis=0)
    values = jnp.dot(rows_enc, w_value[0], preferred_element_type=jnp.float32).astype(jnp.bfloat16)
    lots, values = gather_lots(first, second, values)
    more = place(lots)
    keys = lax.dot_general(
        w_key[0], rows_enc, (((0,), (1,)), ((), ())), preferred_element_type=jnp.float32
    ).astype(jnp.bfloat16)
    span_count = hidden.shape[0] // SPAN
    steps = span_count + SKEW * (sections - 1)
    plan = make_plan(owner[0], section_id, steps, span_count)
    route = [(s, s + 1) for s in range(sections - 1)]
    kept = None
    arrived = [None] * SKEW
    for step in range(steps):
        sent, kept = layer_step(
            step, plan, hidden, arrived[step], mats, more, keys, values, kept
        )
        if step + SKEW < steps:
            arrived.append(lax.ppermute(sent, "section", route))
    return kept[None]


def solution(mesh):
    placed = (
        P("dp", None),
        P("dp", None, None),
        P("dp", None),
        P("section", "dp", None),
        P("section", None, None),
        P("section", None, None),
        P("section", None, "dp"),
    )
    return jax.shard_map(
        per_device, mesh=mesh, in_specs=placed, out_specs=P("section", "dp", None), check_vma=False
    )
```

```python
import functools

import jax
import jax.numpy as jnp
from jax import lax
from jax.experimental import pallas as pl
from jax.experimental.pallas import tpu as pltpu
from jax.sharding import PartitionSpec as P

HEADS = 16
HDIM = 128
SPAN = 64
NBR_LEN = 128
MOST = 4
VMEM_LIMIT = 13 * 1024 * 1024
LOT = 6
KEPT = HEADS - 2 * LOT
RING = 4
CORES = 2
NEAR = [0, -1, 1, 2]
STORES = 4
PAIR = 2
SKEW = 2

epsilon = 1e-05


def pack_kernel(query_ref, out_ref, packed_ref, first_ref, second_ref):
    for head in range(HEADS):
        block = slice(head * HDIM, (head + 1) * HDIM)
        if head < KEPT:
            packed_ref[head] = query_ref[:, block]
        elif head < KEPT + LOT:
            first_ref[head - KEPT] = query_ref[:, block]
        else:
            second_ref[head - KEPT - LOT] = query_ref[:, block]
        packed_ref[KEPT + head] = out_ref[block, :]


def pack(query_shard, out_shard):
    vmem = pl.BlockSpec(memory_space=pltpu.VMEM)
    shapes = [(KEPT + HEADS, HDIM, HDIM), (LOT, HDIM, HDIM), (LOT, HDIM, HDIM)]
    return pl.pallas_call(
        pack_kernel,
        in_specs=[vmem, vmem],
        out_specs=[vmem] * 3,
        out_shape=[jax.ShapeDtypeStruct(shape, query_shard.dtype) for shape in shapes],
    )(query_shard, out_shard)


def shifted(block, x_by, z_by, core_by=0):
    route = []
    for x in range(RING):
        for z in range(RING):
            for core in range(CORES):
                there = ((x + x_by) % RING * RING + (z + z_by) % RING) * CORES + (core ^ core_by)
                route.append(((x * RING + z) * CORES + core, there))
    return lax.ppermute(block, "dp", route)


def around(block, x_by, z_by, meanwhile=None):
    half = block.shape[0] // 2
    behind = shifted(block, x_by, z_by)
    ahead = shifted(block, -x_by, -z_by)
    if meanwhile is not None:
        behind, ahead, meanwhile = lax.optimization_barrier((behind, ahead, meanwhile))
    far_first = shifted(behind[:half], x_by, z_by)
    far_second = shifted(ahead[half:], -x_by, -z_by)
    joined = jnp.concatenate([block, behind, ahead, far_first, far_second], axis=0)
    return joined if meanwhile is None else (joined, meanwhile)


def gather_lots(first, second, meanwhile):
    first_row, second_row = around(first, 1, 0), around(second, 0, 1)
    first_lot, meanwhile = around(first_row, 0, 1, meanwhile)
    lots = [first_lot, around(second_row, 1, 0)]
    lots = [lot.reshape(RING * RING, LOT, HDIM, HDIM) for lot in lots]
    lots = [jnp.concatenate([lot, shifted(lot, 0, 0, 1)], axis=0) for lot in lots]
    return lots, meanwhile


def members_table():
    me = lax.axis_index("dp").astype(jnp.int32)
    x, z, core = me // (RING * CORES), me // CORES % RING, me % CORES
    near = jnp.array(NEAR, jnp.int32)
    x_at, z_at = (x + near + RING) % RING, (z + near + RING) % RING
    first, second = [], []
    for core_by in range(CORES):
        core_at = (core + core_by) % CORES
        first.append((x_at[None, :] * RING + z_at[:, None]) * CORES + core_at)
        second.append((x_at[:, None] * RING + z_at[None, :]) * CORES + core_at)
    return jnp.stack([jnp.stack(rows).reshape(-1) for rows in (first, second)]).astype(jnp.int32)


def step_kernel(
    step, plan, table, hidden_ref, mats, first_lot, second_lot, keys_hbm, values_hbm, *rest,
):
    sent_ref, kept_ref, stream, ordered, queries, scores, attended, keys, values, load_sems, store_sems = rest[-11:]
    members = mats.shape[0]
    depth, width = members * HDIM, HEADS * HDIM
    span_at, active, first = plan[step, 0], plan[step, 1], plan[step, 2]
    window, low, high = plan[step, 3], plan[step, 4], plan[step, 5]
    window_at = pl.ds(pl.multiple_of(window * NBR_LEN, NBR_LEN), MOST * NBR_LEN)
    span_rows = pl.ds(pl.multiple_of(span_at * SPAN, SPAN), SPAN)
    key_copy = pltpu.make_async_copy(keys_hbm.at[:, window_at], keys, load_sems.at[0])
    value_copy = pltpu.make_async_copy(values_hbm.at[window_at, :], values, load_sems.at[1])
    key_copy.start()
    value_copy.start()

    if step < SKEW:
        stream[...] = hidden_ref[span_rows, :]
    else:
        moved_ref = rest[0]

        @pl.when(first == 1)
        def _():
            stream[...] = hidden_ref[span_rows, :]

        @pl.when(first == 0)
        def _():
            stream[...] = moved_ref[...]

    for lot in range(2):
        for member in range(members):
            columns = pl.ds(pl.multiple_of(table[lot, member] * HDIM, HDIM), HDIM)
            ordered[lot, :, member * HDIM : (member + 1) * HDIM] = stream[:, columns]
    wide = stream[...].astype(jnp.float32)
    scale = lax.rsqrt(jnp.mean(wide * wide, axis=1, keepdims=True) + epsilon)
    for head in range(0, HEADS, PAIR):
        lot, at = divmod(head - KEPT, LOT)
        source = (first_lot, second_lot)[lot]
        rows = ordered[lot] if head >= KEPT else stream[...]
        if head < KEPT:
            source, at = mats, head
        matrix = jnp.concatenate(
            [source[:, at + i].reshape(depth, HDIM) for i in range(PAIR)], axis=1
        )
        part = jnp.dot(rows, matrix, preferred_element_type=jnp.float32)
        queries[:, head * HDIM : (head + PAIR) * HDIM] = (part * scale).astype(jnp.bfloat16)
    key_copy.wait()
    for head in range(HEADS):
        columns = slice(head * HDIM, (head + 1) * HDIM)
        scores[head] = jnp.dot(queries[:, columns], keys[columns, :], preferred_element_type=jnp.float32)
    value_copy.wait()
    lane = lax.broadcasted_iota(jnp.int32, (SPAN, MOST * NBR_LEN), 1)
    belongs = (lane >= low * NBR_LEN) & (lane < high * NBR_LEN)
    for head in range(HEADS):
        columns = slice(head * HDIM, (head + 1) * HDIM)
        weights = jnp.where(belongs, jnp.exp(scores[head] * (1.0 / HDIM**0.5)), 0.0)
        weights = weights / jnp.sum(weights, axis=1, keepdims=True)
        attended[:, columns] = jnp.dot(
            weights.astype(jnp.bfloat16), values[:, columns], preferred_element_type=jnp.float32
        ).astype(jnp.bfloat16)
    portion = depth // STORES
    stores = [
        pltpu.make_async_copy(
            sent_ref.at[:, i * portion : (i + 1) * portion],
            kept_ref.at[span_rows, i * portion : (i + 1) * portion],
            store_sems.at[i],
        )
        for i in range(STORES)
    ]
    for member in range(0, members, PAIR):
        matrix = jnp.concatenate(
            [mats[member + i, KEPT:].reshape(width, HDIM) for i in range(PAIR)], axis=1
        )
        branch = jnp.dot(attended[...], matrix, preferred_element_type=jnp.float32)
        columns = slice(member * HDIM, (member + PAIR) * HDIM)
        sent_ref[:, columns] = (stream[:, columns].astype(jnp.float32) + branch).astype(jnp.bfloat16)
        if columns.stop % portion == 0:
            pl.when(active == 1)(stores[columns.stop // portion - 1].start)

    @pl.when(active == 1)
    def _():
        for store in stores:
            store.wait()


def layer_step(step, plan, table, hidden, moved, mats, lots, keys, values, kept):
    model_width, width = hidden.shape[1], values.shape[1]
    vmem = pl.BlockSpec(memory_space=pltpu.VMEM)
    smem = pl.BlockSpec(memory_space=pltpu.SMEM)
    anywhere = pl.BlockSpec(memory_space=pl.ANY)
    work = 2 * SPAN * model_width * width * 2 + 2 * 2 * SPAN * MOST * NBR_LEN * width
    arrived = [] if moved is None else [moved]
    before = [] if kept is None else [kept]
    return pl.pallas_call(
        functools.partial(step_kernel, step),
        in_specs=[smem, smem, vmem, vmem, vmem, vmem, anywhere, anywhere] + [vmem] * len(arrived) + [anywhere] * len(before),
        out_specs=[vmem, anywhere],
        scratch_shapes=[
            pltpu.VMEM((SPAN, model_width), jnp.bfloat16),
            pltpu.VMEM((2, SPAN, model_width), jnp.bfloat16),
            pltpu.VMEM((SPAN, width), jnp.bfloat16),
            pltpu.VMEM((HEADS, SPAN, MOST * NBR_LEN), jnp.float32),
            pltpu.VMEM((SPAN, width), jnp.bfloat16),
            pltpu.VMEM((width, MOST * NBR_LEN), jnp.bfloat16),
            pltpu.VMEM((MOST * NBR_LEN, width), jnp.bfloat16),
            pltpu.SemaphoreType.DMA((2,)),
            pltpu.SemaphoreType.DMA((STORES,)),
        ],
        out_shape=[
            jax.ShapeDtypeStruct((SPAN, model_width), jnp.bfloat16),
            jax.ShapeDtypeStruct(hidden.shape, hidden.dtype),
        ],
        input_output_aliases={8 + len(arrived): 1} if before else {},
        compiler_params=pltpu.CompilerParams(vmem_limit_bytes=VMEM_LIMIT),
        cost_estimate=pl.CostEstimate(
            flops=work,
            bytes_accessed=20 * 1024 * 1024,
            transcendentals=SPAN * MOST * NBR_LEN * HEADS,
        ),
    )(
        plan,
        table,
        pltpu.with_memory_space_constraint(hidden, pltpu.VMEM),
        pltpu.with_memory_space_constraint(mats, pltpu.VMEM),
        *[pltpu.with_memory_space_constraint(lot, pltpu.VMEM) for lot in lots],
        pltpu.with_memory_space_constraint(keys, pltpu.HBM),
        pltpu.with_memory_space_constraint(values, pltpu.HBM),
        *arrived,
        *before,
    )


def make_plan(owners, section_id, steps, span_count):
    span = jnp.arange(steps, dtype=jnp.int32) - SKEW * section_id
    active = ((span >= 0) & (span < span_count)).astype(jnp.int32)
    span = jnp.clip(span, 0, span_count - 1)
    start = jnp.sum((owners[None, :] < span[:, None]).astype(jnp.int32), axis=1)
    count = jnp.sum((owners[None, :] == span[:, None]).astype(jnp.int32), axis=1)
    window = jnp.minimum(start, owners.shape[0] - MOST)
    low = start - window
    first = jnp.broadcast_to((section_id == 0).astype(jnp.int32), span.shape)
    return jnp.stack([span, active, first, window, low, low + count], axis=1).astype(jnp.int32)


def per_device(hidden, encoded, owner, w_query, w_key, w_value, w_out):
    section_id = lax.axis_index("section").astype(jnp.int32)
    sections = lax.axis_size("section")
    rows_enc = encoded.reshape(-1, encoded.shape[2])
    packed, first, second = pack(w_query[0], w_out[0])
    mats = lax.all_gather(packed, "dp", axis=0)
    values = jnp.dot(rows_enc, w_value[0], preferred_element_type=jnp.float32).astype(jnp.bfloat16)
    lots, values = gather_lots(first, second, values)
    table = members_table()
    keys = lax.dot_general(
        w_key[0], rows_enc, (((0,), (1,)), ((), ())), preferred_element_type=jnp.float32
    ).astype(jnp.bfloat16)
    span_count = hidden.shape[0] // SPAN
    steps = span_count + SKEW * (sections - 1)
    plan = make_plan(owner[0], section_id, steps, span_count)
    route = [(s, s + 1) for s in range(sections - 1)]
    kept = None
    arrived = [None] * SKEW
    for step in range(steps):
        sent, kept = layer_step(
            step, plan, table, hidden, arrived[step], mats, lots, keys, values, kept
        )
        if step + SKEW < steps:
            arrived.append(lax.ppermute(sent, "section", route))
    return kept[None]


def solution(mesh):
    placed = (
        P("dp", None),
        P("dp", None, None),
        P("dp", None),
        P("section", "dp", None),
        P("section", None, None),
        P("section", None, None),
        P("section", None, "dp"),
    )
    return jax.shard_map(
        per_device, mesh=mesh, in_specs=placed, out_specs=P("section", "dp", None), check_vma=False
    )
```
